32 devices in a mesh: group: 4 (over y, x), dev: 8 (over z, core).
Axes of the slice: x: 2, y: 2, z: 4, core: 2. Of those that a mesh axis runs over, the one named last changes fastest.
Arguments:
- member_pressure_heads: float32 [192, 128, 768], P('group', 'dev'), may hold values from -4 to 1
- soil_index: int32 [128, 768], P('dev'), may hold values from 0 to 7
- ks_table: float32 [8], replicated, may hold values from 0.05 to 0.5
- alpha_table: float32 [8], replicated, may hold values from 0.5 to 3
- obs_op: float32 [128, 6, 32, 128], P(('dev', 'group')), may hold values from -0.1875 to 0.1875
- obs_mask: int32 [128, 6], P(('dev', 'group')), may hold values from 0 to 1
- obs_values: float32 [128, 6, 32], P(('dev', 'group')), may hold values from -6 to 6
Outputs:
- analysis: float32 [192, 128, 768], P('group', 'dev')
The draws below stay inside these ranges and needn't reach their ends.
All inputs are finite; a program needn't handle non-finite values.
Results may differ from the reference program's by a relative error of at most 0.0003.
Values sent between devices are 32-bit elements; how exact they have to be, the bound alone decides.
A program may use at most 64 MiB of HBM per device.

```python
import math
import jax
import jax.numpy as jnp
from jax import lax

MEMBERS = 192
COLUMNS = 768
OBS_BLOCK = 32
SOIL_TYPES = 8
MODEL_STEPS = 3
NEWTON_STEPS = 12
BLOCKS = 6
GRID_ROWS = 128


def draw_member_pressure_heads(key, part):
    key_base = jax.random.fold_in(key, 11)
    key_scale = jax.random.fold_in(key, 12)
    key_noise = jax.random.fold_in(key, 13)
    key_modes = jax.random.fold_in(key, 14)
    key_loads = jax.random.fold_in(key, 15)
    mode_count = 4
    base_field = jax.random.uniform(key_base, (1, GRID_ROWS, COLUMNS), jnp.float32, -2.5, -0.5)
    member_scale = jnp.exp(jax.random.uniform(key_scale, (MEMBERS, 1, 1), jnp.float32, jnp.log(0.02), jnp.log(0.5)))
    mode_fields = jax.random.normal(key_modes, (mode_count, GRID_ROWS * COLUMNS), jnp.float32)
    loadings = jax.random.normal(key_loads, (MEMBERS, mode_count), jnp.float32)
    shared_part = jnp.dot(loadings, mode_fields, precision=jax.lax.Precision.HIGHEST) / jnp.sqrt(mode_count * 1.0)
    shared_part = shared_part.reshape(MEMBERS, GRID_ROWS, COLUMNS)
    own_part = jax.random.normal(key_noise, (MEMBERS, GRID_ROWS, COLUMNS), jnp.float32)
    share_weight = 0.5
    noise_field = jnp.sqrt(1.0 - share_weight) * own_part + jnp.sqrt(share_weight) * shared_part
    noise_field = jnp.clip(noise_field, -3.0, 3.0)
    return base_field + member_scale * noise_field


def draw_obs_mask(key, part):
    random_draws = jax.random.randint(jax.random.fold_in(key, 23), (GRID_ROWS, BLOCKS), 0, 4 * GRID_ROWS, dtype=jnp.int32)
    thresholds = GRID_ROWS + 2 * jnp.arange(GRID_ROWS, dtype=jnp.int32)
    return (random_draws < thresholds[:, None]).astype(jnp.int32)


def with_ends(values, own_key, least, largest):
    shape = values.shape
    place = [jax.random.randint(jax.random.fold_in(own_key, axis), (), 0, shape[axis]) for axis in range(len(shape))]
    values = values.at[tuple(place)].set(least)
    longest = shape.index(max(shape))
    place[longest] = (place[longest] + 1) % shape[longest]
    return values.at[tuple(place)].set(largest)


def levels(stream_key, extent, shards, smallest, high):
    loudness = 1.0
    for axis_at, blocks in shards:
        steps = jax.random.uniform(jax.random.fold_in(jax.random.fold_in(stream_key, 6), axis_at), (blocks,), jnp.float32, smallest / len(shards), high / len(shards))
        loudness = loudness * jnp.repeat(jnp.exp(steps), extent[axis_at] // blocks).reshape((-1,) + (1,) * (len(extent) - 1 - axis_at))
    return loudness


def noise(key, extent, spread, reach, shards=(), kind=jnp.bfloat16):
    values = spread * jax.random.normal(key, extent, jnp.float32)
    if shards:
        values = values * levels(key, extent, shards, -0.22, 0.18)
    return jnp.clip(values, -reach, reach).astype(kind)


def setup_inputs(seed: int = 0) -> dict:
    splits = jax.random.split(jax.random.key(seed), 8)
    member_pressure_heads = draw_member_pressure_heads(jax.random.fold_in(splits[7], 71), 0)
    soil_index = with_ends(jax.random.randint(splits[1], (GRID_ROWS, COLUMNS), 0, SOIL_TYPES), jax.random.fold_in(splits[1], 1), 0, SOIL_TYPES - 1).astype(jnp.int32)
    ks_table = jnp.clip(jnp.exp(jax.random.uniform(splits[2], (SOIL_TYPES,), jnp.float32, math.log(0.05), math.log(0.5))), 0.05, 0.5)
    alpha_table = jnp.clip(jnp.exp(jax.random.uniform(splits[3], (SOIL_TYPES,), jnp.float32, math.log(0.5), math.log(3.0))), 0.5, 3.0)
    obs_op = noise(splits[4], (GRID_ROWS, BLOCKS, OBS_BLOCK, 128), (128 * max(1, GRID_ROWS * BLOCKS * OBS_BLOCK // (16 * MEMBERS))) ** -0.5, 0.1875, ((0, 32),), jnp.float32)
    obs_mask = draw_obs_mask(jax.random.fold_in(splits[7], 71), 0)
    obs_values = noise(splits[6], (GRID_ROWS, BLOCKS, OBS_BLOCK), 1.0, 6.0, ((0, 32),), jnp.float32)
    return dict(member_pressure_heads=member_pressure_heads, soil_index=soil_index, ks_table=ks_table, alpha_table=alpha_table, obs_op=obs_op, obs_mask=obs_mask, obs_values=obs_values)


step_duration = 0.1
gravity_head = 1.0
highest = lax.Precision.HIGHEST

def soil_values(soil_index, ks_table, alpha_table):
    soil_kinds = jnp.arange(SOIL_TYPES, dtype=jnp.int32)
    one_hot = (soil_index[None] == soil_kinds[:, None, None]).astype(jnp.float32)
    hydraulic_conductance = lax.optimization_barrier(jnp.sum(one_hot * ks_table[:, None, None], axis=0))
    retention_shape = lax.optimization_barrier(jnp.sum(one_hot * alpha_table[:, None, None], axis=0))
    return (hydraulic_conductance, retention_shape)

def soil_hydraulic_law(heads_now, hydraulic_conductance, retention_shape):
    factor = jnp.exp(retention_shape * jnp.minimum(heads_now, 0.0))
    return (hydraulic_conductance * factor, 0.1 + 0.4 * retention_shape * factor)

def surface_recharge(padded_heads, padded_k):
    middle = padded_heads[:, 1:-1]
    k_middle = padded_k[:, 1:-1]
    across = 0.5 * (k_middle + padded_k[:, 2:]) * (padded_heads[:, 2:] - middle)
    across = across + 0.5 * (k_middle + padded_k[:, :-2]) * (padded_heads[:, :-2] - middle)
    k_face = 0.5 * (k_middle[..., 1:] + k_middle[..., :-1])
    vertical = k_face * (middle[..., 1:] - middle[..., :-1] - gravity_head)
    border = jnp.zeros_like(middle[..., :1])
    return across + jnp.concatenate([vertical, border], -1) - jnp.concatenate([border, vertical], -1)

def newton_weights(gram_matrix, gram_rhs):
    order_m = gram_matrix.shape[0]
    identity_m = jnp.eye(order_m, dtype=jnp.float32)
    norm_total = jnp.sum(jnp.abs(gram_matrix))

    def one_turn(counter, iterate_pair):
        iterate, inverse = iterate_pair
        middle = 0.5 * (3.0 * identity_m - jnp.dot(inverse, iterate, precision=highest, preferred_element_type=jnp.float32))
        return (jnp.dot(iterate, middle, precision=highest, preferred_element_type=jnp.float32), jnp.dot(middle, inverse, precision=highest, preferred_element_type=jnp.float32))
    iterate, inverse = lax.fori_loop(0, NEWTON_STEPS, one_turn, (gram_matrix / norm_total, identity_m))
    inner_w = jnp.dot(inverse, gram_rhs, precision=highest, preferred_element_type=jnp.float32)
    shift_w = jnp.dot(inverse, inner_w, precision=highest, preferred_element_type=jnp.float32) / norm_total
    return jnp.sqrt((order_m - 1.0) / norm_total) * inverse + shift_w[:, None]

def reference(member_pressure_heads, soil_index, ks_table, alpha_table, obs_op, obs_mask, obs_values):
    hydraulic_conductance, retention_shape = soil_values(soil_index, ks_table, alpha_table)
    predict_heads = member_pressure_heads
    layer_widths = ((0, 0), (1, 1), (0, 0))
    for counter in range(MODEL_STEPS):
        conductivity_field, moisture_capacity = soil_hydraulic_law(predict_heads, hydraulic_conductance, retention_shape)
        predict_heads = predict_heads + step_duration * surface_recharge(jnp.pad(predict_heads, layer_widths), jnp.pad(conductivity_field, layer_widths)) / moisture_capacity
    ensemble_average = lax.optimization_barrier(jnp.mean(predict_heads, axis=0))
    member_anomalies = predict_heads - ensemble_average
    mask_float = obs_mask.astype(jnp.float32)
    masked_op = obs_op * mask_float[:, :, None, None]
    projected = jnp.einsum('rboc,mrbc->rbom', masked_op, member_anomalies.reshape(MEMBERS, GRID_ROWS, BLOCKS, 128), precision=highest).reshape(-1, MEMBERS)
    innovation = (obs_values * mask_float[:, :, None] - jnp.einsum('rboc,rbc->rbo', masked_op, ensemble_average.reshape(GRID_ROWS, BLOCKS, 128), precision=highest)).reshape(-1)
    identity_m = jnp.eye(MEMBERS, dtype=jnp.float32)
    gram_matrix = jnp.dot(projected.T, projected, precision=highest, preferred_element_type=jnp.float32) + (MEMBERS - 1.0) * identity_m
    gram_rhs = jnp.dot(projected.T, innovation, precision=highest, preferred_element_type=jnp.float32)
    mixing = newton_weights(gram_matrix, gram_rhs)
    mixed = jnp.dot(mixing.T, member_anomalies.reshape(MEMBERS, -1), precision=highest, preferred_element_type=jnp.float32)
    return mixed.reshape(MEMBERS, GRID_ROWS, COLUMNS)
```

```python
import functools

import jax
import jax.numpy as jnp
from jax import lax
from jax.experimental import pallas as pl
from jax.experimental.pallas import tpu as pltpu
from jax.sharding import PartitionSpec as P

MODEL_STEPS = 3
NEWTON_STEPS = 12
LANES = 128
SUBLANES = 8

step_duration = 0.1
gravity_head = 1.0
highest = lax.Precision.HIGHEST
MESH = pl.DeviceIdType.MESH
last_dims = (((1,), (1,)), ((), ()))


def soil_values(soil_index, ks_table, alpha_table):
    soil_kinds = jnp.arange(ks_table.shape[0], dtype=jnp.int32)
    one_hot = (soil_index[None] == soil_kinds[:, None, None]).astype(jnp.float32)
    return jnp.stack(
        [
            jnp.sum(one_hot * ks_table[:, None, None], axis=0),
            jnp.sum(one_hot * alpha_table[:, None, None], axis=0),
        ],
        axis=1,
    )


def place(group, dev):
    return {"group": group, "dev": dev}


def forecast_kernel(
    groups, devs, heads, soil, obs, fc, proj,
    ext_a, ext_b, soil_ext, obs_all,
    local_sem, obs_send, obs_recv, halo_send, halo_recv, soil_send, soil_recv,
):
    w = MODEL_STEPS
    rows, members, columns = heads.shape
    blocks = columns // LANES
    server_rows = rows // groups
    g = lax.axis_index("group")
    d = lax.axis_index("dev")
    first, last = d == 0, d == devs - 1

    own_heads = pltpu.make_async_copy(heads, ext_a.at[pl.ds(w, rows)], local_sem.at[0])
    own_soil = pltpu.make_async_copy(soil, soil_ext.at[pl.ds(w, rows)], local_sem.at[1])
    own_obs = pltpu.make_async_copy(obs, obs_all.at[g], local_sem.at[2])
    own_heads.start()
    own_soil.start()
    own_obs.start()

    barrier = pltpu.get_barrier_semaphore()
    for k in range(1, groups):
        pl.semaphore_signal(
            barrier, inc=1, device_id=place((g + k) % groups, d), device_id_type=MESH
        )

    @pl.when(d > 0)
    def _():
        pl.semaphore_signal(barrier, inc=1, device_id=place(g, d - 1), device_id_type=MESH)

    @pl.when(d < devs - 1)
    def _():
        pl.semaphore_signal(barrier, inc=1, device_id=place(g, d + 1), device_id_type=MESH)

    neighbours = (d > 0).astype(jnp.int32) + (d < devs - 1).astype(jnp.int32)
    pl.semaphore_wait(barrier, groups - 1 + neighbours)

    def halo(source, target, send, recv, side):
        start, put, to = ((0, w + rows, d - 1), (rows - w, 0, d + 1))[side]
        return pltpu.make_async_remote_copy(
            src_ref=source.at[pl.ds(start, w)],
            dst_ref=target.at[pl.ds(put, w)],
            send_sem=send.at[side],
            recv_sem=recv.at[side],
            device_id=place(g, to),
            device_id_type=MESH,
        )

    def halos(side):
        return (
            halo(soil, soil_ext, soil_send, soil_recv, side),
            halo(heads, ext_a, halo_send, halo_recv, side),
        )

    @pl.when(d > 0)
    def _():
        for c in halos(0):
            c.start()

    @pl.when(d < devs - 1)
    def _():
        for c in halos(1):
            c.start()

    def obs_copy(k):
        return pltpu.make_async_remote_copy(
            src_ref=obs,
            dst_ref=obs_all.at[g],
            send_sem=obs_send.at[k],
            recv_sem=obs_recv.at[k],
            device_id=place((g + k) % groups, d),
            device_id_type=MESH,
        )

    def obs_arrival(k):
        return pltpu.make_async_remote_copy(
            src_ref=obs,
            dst_ref=obs_all.at[(g + groups - k) % groups],
            send_sem=obs_send.at[k],
            recv_sem=obs_recv.at[k],
            device_id=place((g + k) % groups, d),
            device_id_type=MESH,
        )

    for k in range(1, groups):
        obs_copy(k).start()

    def advance(src, dst, out_shift, low, high):
        def chunk(c, carry):
            part = pl.ds(pl.multiple_of(c * SUBLANES, SUBLANES), SUBLANES)
            shape = (SUBLANES, columns)
            lane = lax.broadcasted_iota(jnp.int32, shape, 1)
            has_next = lane < columns - 1
            has_before = lane > 0

            def law(i):
                h = src[i, part, :]
                ks = jnp.broadcast_to(soil_ext[i, 0:1, :], shape)
                alpha = jnp.broadcast_to(soil_ext[i, 1:2, :], shape)
                factor = jnp.exp(alpha * jnp.minimum(h, 0.0))
                return h, ks * factor, 0.1 + 0.4 * alpha * factor

            def across(h, k, h_next, k_next):
                return 0.5 * (k + k_next) * (h_next - h)

            h0, k0, _ = law(low - 1)
            h1, k1, c1 = law(low)

            def row(i, state):
                h, k, cap, g_before = state
                h_next, k_next, cap_next = law(i + 1)
                g_now = across(h, k, h_next, k_next)
                h_right = pltpu.roll(h, columns - 1, 1)
                k_right = pltpu.roll(k, columns - 1, 1)
                f = 0.5 * (k + k_right) * (h_right - h - gravity_head)
                f = jnp.where(has_next, f, 0.0)
                f_left = pltpu.roll(f, 1, 1)
                inflow = (g_now - g_before) + (f - f_left)
                dst[i - out_shift, part, :] = h + step_duration * inflow / cap
                return h_next, k_next, cap_next, g_now

            lax.fori_loop(low, high, row, (h1, k1, c1, across(h0, k0, h1, k1)))
            return carry

        lax.fori_loop(0, members // SUBLANES, chunk, 0)

    def clear(ref, low, high):
        ref[low:high] = jnp.zeros((high - low,) + ref.shape[1:], jnp.float32)

    own_heads.wait()
    own_soil.wait()

    advance(ext_a, ext_b, 0, w + 1, w + rows - 1)

    @pl.when(d > 0)
    def _():
        for c in halos(0):
            c.wait_send()
        for c in halos(1):
            c.wait_recv()

    @pl.when(d < devs - 1)
    def _():
        for c in halos(1):
            c.wait_send()
        for c in halos(0):
            c.wait_recv()

    @pl.when(first)
    def _():
        clear(ext_a, 0, w)
        clear(soil_ext, 0, w)

    @pl.when(last)
    def _():
        clear(ext_a, w + rows, rows + 2 * w)
        clear(soil_ext, w + rows, rows + 2 * w)

    advance(ext_a, ext_b, 0, 1, w + 1)
    advance(ext_a, ext_b, 0, w + rows - 1, rows + 2 * w - 1)

    def outside(ref, low, high):
        @pl.when(first)
        def _():
            clear(ref, low, w)

        @pl.when(last)
        def _():
            clear(ref, w + rows, high)

    outside(ext_b, 1, rows + 2 * w - 1)
    advance(ext_b, ext_a, 0, 2, rows + 2 * w - 2)
    outside(ext_a, 2, rows + 2 * w - 2)
    advance(ext_a, fc, w, w, w + rows)

    own_obs.wait()
    for k in range(1, groups):
        obs_copy(k).wait_send()
        obs_arrival(k).wait_recv()

    width = obs_all.shape[1] // server_rows
    per_block = width // blocks
    pairs = 2
    halves = server_rows // pairs

    def project(t, carry):
        owner, half = t // halves, t % halves
        pieces = []
        for p in range(pairs):
            r = t * pairs + p
            for b in range(blocks):
                weights = obs_all[
                    owner,
                    pl.ds(
                        pl.multiple_of(((half * pairs + p) * blocks + b) * per_block, SUBLANES),
                        per_block,
                    ),
                    :,
                ]
                pieces.append(
                    lax.dot_general(
                        fc[r, :, b * LANES : (b + 1) * LANES],
                        weights,
                        last_dims,
                        precision=highest,
                        preferred_element_type=jnp.float32,
                    )
                )
        proj[owner, :, pl.ds(pl.multiple_of(half * pairs * width, LANES), pairs * width)] = (
            jnp.concatenate(pieces, axis=1)
        )
        return carry

    lax.fori_loop(0, rows // pairs, project, 0)


def analysis_kernel(
    groups, devs, proj, fc, values, res,
    proj_all, gath, part, recv_a, red, recv_b, tot, full, mix, send_buf,
    local_sem, proj_send, proj_recv, fc_send, fc_recv,
    a_send, a_recv, b_send, b_recv, c_send, c_recv, out_send, out_recv,
):
    g = lax.axis_index("group")
    d = lax.axis_index("dev")
    cores = 2
    levels = devs // cores
    z, core = d // cores, d % cores
    teams = groups * cores
    me = g * cores + core
    _, server_rows, share, columns = fc.shape
    members = groups * share
    chunk = members // teams

    own_fc = pltpu.make_async_copy(
        fc.at[g], gath.at[:, pl.ds(pl.multiple_of(g * share, SUBLANES), share), :], local_sem.at[0]
    )
    own_proj = pltpu.make_async_copy(proj.at[g], proj_all.at[g], local_sem.at[1])
    own_fc.start()
    own_proj.start()

    def team(k):
        q = (me + k) % teams
        return q, place(q // cores, z * cores + q % cores)

    barrier = pltpu.get_barrier_semaphore()
    for k in range(1, teams):
        pl.semaphore_signal(barrier, inc=1, device_id=team(k)[1], device_id_type=MESH)
    for k in range(1, levels):
        pl.semaphore_signal(
            barrier,
            inc=1,
            device_id=place(g, (z + k) % levels * cores + core),
            device_id_type=MESH,
        )
    pl.semaphore_wait(barrier, teams - 1 + levels - 1)

    def copy(src, dst, send, recv, to):
        return pltpu.make_async_remote_copy(
            src_ref=src, dst_ref=dst, send_sem=send, recv_sem=recv,
            device_id=to, device_id_type=MESH,
        )

    def peer(k):
        p = (g + k) % groups
        return p, place(p, d)

    def member_slot(p):
        return gath.at[:, pl.ds(pl.multiple_of(p * share, SUBLANES), share), :]

    def proj_copy(k, incoming):
        p, to = peer(k)
        slot = (g + groups - k) % groups if incoming else g
        return copy(proj.at[p], proj_all.at[slot], proj_send.at[k], proj_recv.at[k], to)

    def fc_copy(k, incoming):
        p, to = peer(k)
        slot = (g + groups - k) % groups if incoming else g
        return copy(fc.at[p], member_slot(slot), fc_send.at[k], fc_recv.at[k], to)

    for k in range(1, groups):
        proj_copy(k, False).start()
    for k in range(1, groups):
        fc_copy(k, False).start()
    own_proj.wait()
    for k in range(1, groups):
        proj_copy(k, True).wait_recv()

    observed = jnp.concatenate([proj_all[q] for q in range(groups)], axis=0)
    average = jnp.sum(observed, axis=0, keepdims=True) / members
    centred = observed - average
    innovation = values[...] - average
    extra = full.shape[2] - members
    padding = jnp.concatenate(
        [innovation, jnp.zeros((extra - 1, innovation.shape[1]), jnp.float32)], axis=0
    )
    gram_part = lax.dot_general(
        centred,
        jnp.concatenate([centred, padding], axis=0),
        last_dims,
        precision=highest,
        preferred_element_type=jnp.float32,
    )
    for q in range(teams):
        part[q] = gram_part[q * chunk : (q + 1) * chunk, :]

    def a_copy(k, incoming):
        q, to = team(k)
        slot = (me + teams - k) % teams if incoming else me
        return copy(part.at[q], recv_a.at[slot], a_send.at[k], a_recv.at[k], to)

    for k in range(1, teams):
        a_copy(k, False).start()
    total = part[me]
    for k in range(1, teams):
        a_copy(k, True).wait_recv()
        total = total + recv_a[(me + teams - k) % teams]
    red[...] = total
    recv_b[z] = total

    def b_copy(k, incoming):
        to = place(g, (z + k) % levels * cores + core)
        slot = (z + levels - k) % levels if incoming else z
        return copy(red, recv_b.at[slot], b_send.at[k], b_recv.at[k], to)

    for k in range(1, levels):
        b_copy(k, False).start()
    for k in range(1, levels):
        b_copy(k, True).wait_recv()
    total = recv_b[0]
    for q in range(1, levels):
        total = total + recv_b[q]
    tot[...] = total
    full[me] = total

    def c_copy(k, incoming):
        _, to = team(k)
        slot = (me + teams - k) % teams if incoming else me
        return copy(tot, full.at[slot], c_send.at[k], c_recv.at[k], to)

    for k in range(1, teams):
        c_copy(k, False).start()
    for k in range(1, teams):
        c_copy(k, True).wait_recv()

    summed = jnp.concatenate([full[q] for q in range(teams)], axis=0)
    square = (members, members)
    diagonal = lax.broadcasted_iota(jnp.int32, square, 0) == lax.broadcasted_iota(
        jnp.int32, square, 1
    )
    identity = jnp.where(diagonal, 1.0, 0.0).astype(jnp.float32)
    gram = summed[:, :members] + (members - 1.0) * identity
    rhs = summed[:, members : members + 1]
    norm_total = jnp.sum(jnp.abs(gram))

    def dot(a, b):
        return jnp.dot(a, b, precision=highest, preferred_element_type=jnp.float32)

    def turn(_, pair):
        iterate, inverse = pair
        middle = 0.5 * (3.0 * identity - dot(inverse, iterate))
        return dot(iterate, middle), dot(middle, inverse)

    _, inverse = lax.fori_loop(0, NEWTON_STEPS, turn, (gram / norm_total, identity))
    right = jnp.broadcast_to(rhs, (members, LANES))
    shift = dot(inverse, dot(inverse, right)) / norm_total
    mix[...] = (jnp.sqrt((members - 1.0) / norm_total) * inverse + shift[:, 0:1]).T

    own_fc.wait()
    for k in range(1, groups):
        fc_copy(k, True).wait_recv()

    def centre(s, carry):
        block = gath[s]
        gath[s] = block - jnp.sum(block, axis=0, keepdims=True) / members
        return carry

    lax.fori_loop(0, server_rows, centre, 0)

    def out_copy(k, s, incoming):
        p, to = peer(k)
        slot = (g + groups - k) % groups if incoming else g
        return copy(
            send_buf.at[k, s], res.at[slot, s], out_send.at[k, s], out_recv.at[k, s], to
        )

    def mixed(p, s):
        weights = mix[pl.ds(pl.multiple_of(p * share, SUBLANES), share), :]
        return dot(weights, gath[s])

    for k in range(1, groups):

        def send(s, carry):
            send_buf[k, s] = mixed(peer(k)[0], s)
            out_copy(k, s, False).start()
            return carry

        lax.fori_loop(0, server_rows, send, 0)

    def keep(s, carry):
        res[g, s] = mixed(g, s)
        return carry

    lax.fori_loop(0, server_rows, keep, 0)

    for k in range(1, groups):
        proj_copy(k, False).wait_send()
        fc_copy(k, False).wait_send()
    for k in range(1, teams):
        a_copy(k, False).wait_send()
        c_copy(k, False).wait_send()
    for k in range(1, levels):
        b_copy(k, False).wait_send()
    for k in range(1, groups):
        for s in range(server_rows):
            out_copy(k, s, False).wait_send()
            out_copy(k, s, True).wait_recv()


def body(groups, devs, heads, soil_index, ks_table, alpha_table, obs_op, obs_mask, obs_values):
    soil = soil_values(soil_index, ks_table, alpha_table)
    mask = obs_mask.astype(jnp.float32)
    weights = (obs_op * mask[:, :, None, None]).reshape(-1, obs_op.shape[-1])
    values = (obs_values * mask[:, :, None]).reshape(1, -1)
    share, rows, columns = heads.shape
    server_rows = rows // groups
    observations = weights.shape[0]
    members = groups * share
    vmem = pl.BlockSpec(memory_space=pltpu.VMEM)
    anywhere = pl.BlockSpec(memory_space=pl.ANY)
    dma = pltpu.SemaphoreType.DMA
    f32 = jnp.float32
    extended = rows + 2 * MODEL_STEPS

    fc, proj = pl.pallas_call(
        functools.partial(forecast_kernel, groups, devs),
        out_shape=(
            jax.ShapeDtypeStruct((rows, share, columns), f32),
            jax.ShapeDtypeStruct((groups, share, observations), f32),
        ),
        in_specs=[anywhere] * 3,
        out_specs=(vmem, vmem),
        scratch_shapes=[
            pltpu.VMEM((extended, share, columns), f32),
            pltpu.VMEM((extended, share, columns), f32),
            pltpu.VMEM((extended, 2, columns), f32),
            pltpu.VMEM((groups, observations, LANES), f32),
            dma((3,)),
            dma((groups,)),
            dma((groups,)),
            dma((2,)),
            dma((2,)),
            dma((2,)),
            dma((2,)),
        ],
        compiler_params=pltpu.CompilerParams(collective_id=0, has_side_effects=True),
        name="forecast",
    )(heads.transpose(1, 0, 2), soil, weights)

    cores = 2
    teams, levels = groups * cores, devs // cores
    chunk = members // teams
    wide = (members // LANES + 1) * LANES
    res = pl.pallas_call(
        functools.partial(analysis_kernel, groups, devs),
        out_shape=jax.ShapeDtypeStruct((groups, server_rows, share, columns), f32),
        in_specs=[anywhere, anywhere, vmem],
        out_specs=vmem,
        scratch_shapes=[
            pltpu.VMEM((groups, share, observations), f32),
            pltpu.VMEM((server_rows, members, columns), f32),
            pltpu.VMEM((teams, chunk, wide), f32),
            pltpu.VMEM((teams, chunk, wide), f32),
            pltpu.VMEM((chunk, wide), f32),
            pltpu.VMEM((levels, chunk, wide), f32),
            pltpu.VMEM((chunk, wide), f32),
            pltpu.VMEM((teams, chunk, wide), f32),
            pltpu.VMEM((members, members), f32),
            pltpu.VMEM((groups, server_rows, share, columns), f32),
            dma((2,)),
            dma((groups,)),
            dma((groups,)),
            dma((groups,)),
            dma((groups,)),
            dma((teams,)),
            dma((teams,)),
            dma((levels,)),
            dma((levels,)),
            dma((teams,)),
            dma((teams,)),
            dma((groups, server_rows)),
            dma((groups, server_rows)),
        ],
        compiler_params=pltpu.CompilerParams(collective_id=1, has_side_effects=True),
        name="analysis",
    )(proj, fc.reshape(groups, server_rows, share, columns), values)
    return res.reshape(rows, share, columns).transpose(1, 0, 2)


def solution(mesh):
    groups, devs = mesh.shape["group"], mesh.shape["dev"]
    placed = (
        P("group", "dev", None),
        P("dev", None),
        P(),
        P(),
        P(("dev", "group"), None, None, None),
        P(("dev", "group"), None),
        P(("dev", "group"), None, None),
    )
    return jax.shard_map(
        functools.partial(body, groups, devs),
        mesh=mesh,
        in_specs=placed,
        out_specs=P("group", "dev", None),
        check_vma=False,
    )
```

```python
import functools

import jax
import jax.numpy as jnp
from jax import lax
from jax.experimental import pallas as pl
from jax.experimental.pallas import tpu as pltpu
from jax.sharding import PartitionSpec as P

MODEL_STEPS = 3
NEWTON_STEPS = 12
LANES = 128
SUBLANES = 8

step_duration = 0.1
gravity_head = 1.0
highest = lax.Precision.HIGHEST
MESH = pl.DeviceIdType.MESH
last_dims = (((1,), (1,)), ((), ()))


def soil_values(soil_index, ks_table, alpha_table):
    soil_kinds = jnp.arange(ks_table.shape[0], dtype=jnp.int32)
    one_hot = (soil_index[None] == soil_kinds[:, None, None]).astype(jnp.float32)
    return jnp.stack(
        [
            jnp.sum(one_hot * ks_table[:, None, None], axis=0),
            jnp.sum(one_hot * alpha_table[:, None, None], axis=0),
        ],
        axis=1,
    )


def place(group, dev):
    return {"group": group, "dev": dev}


def forecast_kernel(
    groups, devs, heads, soil, obs, fc, proj,
    ext_a, ext_b, soil_ext, obs_all,
    local_sem, obs_send, obs_recv, halo_send, halo_recv, soil_send, soil_recv,
):
    w = MODEL_STEPS
    rows, members, columns = heads.shape
    blocks = columns // LANES
    server_rows = rows // groups
    g = lax.axis_index("group")
    d = lax.axis_index("dev")
    first, last = d == 0, d == devs - 1

    own_heads = pltpu.make_async_copy(heads, ext_a.at[pl.ds(w, rows)], local_sem.at[0])
    own_soil = pltpu.make_async_copy(soil, soil_ext.at[pl.ds(w, rows)], local_sem.at[1])
    own_obs = pltpu.make_async_copy(obs, obs_all.at[g], local_sem.at[2])
    own_heads.start()
    own_soil.start()
    own_obs.start()

    barrier = pltpu.get_barrier_semaphore()
    for k in range(1, groups):
        pl.semaphore_signal(
            barrier, inc=1, device_id=place((g + k) % groups, d), device_id_type=MESH
        )

    @pl.when(d > 0)
    def _():
        pl.semaphore_signal(barrier, inc=1, device_id=place(g, d - 1), device_id_type=MESH)

    @pl.when(d < devs - 1)
    def _():
        pl.semaphore_signal(barrier, inc=1, device_id=place(g, d + 1), device_id_type=MESH)

    neighbours = (d > 0).astype(jnp.int32) + (d < devs - 1).astype(jnp.int32)
    pl.semaphore_wait(barrier, groups - 1 + neighbours)

    def halo(source, target, send, recv, side):
        start, put, to = ((0, w + rows, d - 1), (rows - w, 0, d + 1))[side]
        return pltpu.make_async_remote_copy(
            src_ref=source.at[pl.ds(start, w)],
            dst_ref=target.at[pl.ds(put, w)],
            send_sem=send.at[side],
            recv_sem=recv.at[side],
            device_id=place(g, to),
            device_id_type=MESH,
        )

    def halos(side):
        return (
            halo(soil, soil_ext, soil_send, soil_recv, side),
            halo(heads, ext_a, halo_send, halo_recv, side),
        )

    @pl.when(d > 0)
    def _():
        for c in halos(0):
            c.start()

    @pl.when(d < devs - 1)
    def _():
        for c in halos(1):
            c.start()

    def obs_copy(k):
        return pltpu.make_async_remote_copy(
            src_ref=obs,
            dst_ref=obs_all.at[g],
            send_sem=obs_send.at[k],
            recv_sem=obs_recv.at[k],
            device_id=place((g + k) % groups, d),
            device_id_type=MESH,
        )

    def obs_arrival(k):
        return pltpu.make_async_remote_copy(
            src_ref=obs,
            dst_ref=obs_all.at[(g + groups - k) % groups],
            send_sem=obs_send.at[k],
            recv_sem=obs_recv.at[k],
            device_id=place((g + k) % groups, d),
            device_id_type=MESH,
        )

    for k in range(1, groups):
        obs_copy(k).start()

    def advance(src, dst, out_shift, low, high):
        def chunk(c, carry):
            part = pl.ds(pl.multiple_of(c * SUBLANES, SUBLANES), SUBLANES)
            shape = (SUBLANES, columns)
            lane = lax.broadcasted_iota(jnp.int32, shape, 1)
            has_next = lane < columns - 1
            has_before = lane > 0

            def law(i):
                h = src[i, part, :]
                ks = jnp.broadcast_to(soil_ext[i, 0:1, :], shape)
                alpha = jnp.broadcast_to(soil_ext[i, 1:2, :], shape)
                factor = jnp.exp(alpha * jnp.minimum(h, 0.0))
                return h, ks * factor, 0.1 + 0.4 * alpha * factor

            def across(h, k, h_next, k_next):
                return 0.5 * (k + k_next) * (h_next - h)

            h0, k0, _ = law(low - 1)
            h1, k1, c1 = law(low)

            def row(i, state):
                h, k, cap, g_before = state
                h_next, k_next, cap_next = law(i + 1)
                g_now = across(h, k, h_next, k_next)
                h_right = pltpu.roll(h, columns - 1, 1)
                k_right = pltpu.roll(k, columns - 1, 1)
                f = 0.5 * (k + k_right) * (h_right - h - gravity_head)
                f = jnp.where(has_next, f, 0.0)
                f_left = 0.5 * (k + pltpu.roll(k, 1, 1)) * (h - pltpu.roll(h, 1, 1) - gravity_head)
                f_left = jnp.where(has_before, f_left, 0.0)
                inflow = (g_now - g_before) + (f - f_left)
                dst[i - out_shift, part, :] = h + step_duration * inflow / cap
                return h_next, k_next, cap_next, g_now

            lax.fori_loop(low, high, row, (h1, k1, c1, across(h0, k0, h1, k1)), unroll=2)
            return carry

        lax.fori_loop(0, members // SUBLANES, chunk, 0)

    def clear(ref, low, high):
        ref[low:high] = jnp.zeros((high - low,) + ref.shape[1:], jnp.float32)

    own_heads.wait()
    own_soil.wait()

    advance(ext_a, ext_b, 0, w + 1, w + rows - 1)

    @pl.when(d > 0)
    def _():
        for c in halos(0):
            c.wait_send()
        for c in halos(1):
            c.wait_recv()

    @pl.when(d < devs - 1)
    def _():
        for c in halos(1):
            c.wait_send()
        for c in halos(0):
            c.wait_recv()

    @pl.when(first)
    def _():
        clear(ext_a, 0, w)
        clear(soil_ext, 0, w)

    @pl.when(last)
    def _():
        clear(ext_a, w + rows, rows + 2 * w)
        clear(soil_ext, w + rows, rows + 2 * w)

    advance(ext_a, ext_b, 0, 1, w + 1)
    advance(ext_a, ext_b, 0, w + rows - 1, rows + 2 * w - 1)

    def outside(ref, low, high):
        @pl.when(first)
        def _():
            clear(ref, low, w)

        @pl.when(last)
        def _():
            clear(ref, w + rows, high)

    outside(ext_b, 1, rows + 2 * w - 1)
    advance(ext_b, ext_a, 0, 2, rows + 2 * w - 2)
    outside(ext_a, 2, rows + 2 * w - 2)
    advance(ext_a, fc, w, w, w + rows)

    own_obs.wait()
    for k in range(1, groups):
        obs_copy(k).wait_send()
        obs_arrival(k).wait_recv()

    width = obs_all.shape[1] // server_rows
    per_block = width // blocks
    pairs = 2
    halves = server_rows // pairs

    def project(t, carry):
        owner, half = t // halves, t % halves
        pieces = []
        for p in range(pairs):
            r = t * pairs + p
            for b in range(blocks):
                weights = obs_all[
                    owner,
                    pl.ds(
                        pl.multiple_of(((half * pairs + p) * blocks + b) * per_block, SUBLANES),
                        per_block,
                    ),
                    :,
                ]
                pieces.append(
                    lax.dot_general(
                        fc[r, :, b * LANES : (b + 1) * LANES],
                        weights,
                        last_dims,
                        precision=highest,
                        preferred_element_type=jnp.float32,
                    )
                )
        proj[owner, :, pl.ds(pl.multiple_of(half * pairs * width, LANES), pairs * width)] = (
            jnp.concatenate(pieces, axis=1)
        )
        return carry

    lax.fori_loop(0, rows // pairs, project, 0)


def analysis_kernel(
    groups, devs, proj, fc, values, res,
    proj_all, gath, part, recv_a, red, recv_b, tot, full, mix, send_buf,
    local_sem, proj_send, proj_recv, fc_send, fc_recv,
    a_send, a_recv, b_send, b_recv, c_send, c_recv, out_send, out_recv,
):
    g = lax.axis_index("group")
    d = lax.axis_index("dev")
    _, server_rows, share, columns = fc.shape
    members = groups * share
    chunk = members // devs

    own_fc = pltpu.make_async_copy(
        fc.at[g], gath.at[:, pl.ds(pl.multiple_of(g * share, SUBLANES), share), :], local_sem.at[0]
    )
    own_proj = pltpu.make_async_copy(proj.at[g], proj_all.at[g], local_sem.at[1])
    own_fc.start()
    own_proj.start()

    barrier = pltpu.get_barrier_semaphore()
    for k in range(1, groups):
        pl.semaphore_signal(
            barrier, inc=1, device_id=place((g + k) % groups, d), device_id_type=MESH
        )
    for k in range(1, devs):
        pl.semaphore_signal(
            barrier, inc=1, device_id=place(g, (d + k) % devs), device_id_type=MESH
        )
    pl.semaphore_wait(barrier, groups - 1 + devs - 1)

    def copy(src, dst, send, recv, to):
        return pltpu.make_async_remote_copy(
            src_ref=src, dst_ref=dst, send_sem=send, recv_sem=recv,
            device_id=to, device_id_type=MESH,
        )

    def peer(k):
        p = (g + k) % groups
        return p, place(p, d)

    def member_slot(p, s):
        return gath.at[s, pl.ds(pl.multiple_of(p * share, SUBLANES), share), :]

    def proj_copy(k, incoming):
        p, to = peer(k)
        slot = (g + groups - k) % groups if incoming else g
        return copy(proj.at[p], proj_all.at[slot], proj_send.at[k], proj_recv.at[k], to)

    def fc_copy(k, s, incoming):
        p, to = peer(k)
        slot = (g + groups - k) % groups if incoming else g
        return copy(fc.at[p, s], member_slot(slot, s), fc_send.at[k, s], fc_recv.at[k, s], to)

    for k in range(1, groups):
        proj_copy(k, False).start()
    for k in range(1, groups):
        fc_copy(k, 0, False).start()
    own_proj.wait()
    for k in range(1, groups):
        proj_copy(k, True).wait_recv()

    observed = jnp.concatenate([proj_all[q] for q in range(groups)], axis=0)
    average = jnp.sum(observed, axis=0, keepdims=True) / members
    centred = observed - average
    innovation = values[...] - average
    extra = full.shape[2] - members
    padding = jnp.concatenate(
        [innovation, jnp.zeros((extra - 1, innovation.shape[1]), jnp.float32)], axis=0
    )
    gram_part = lax.dot_general(
        centred,
        jnp.concatenate([centred, padding], axis=0),
        last_dims,
        precision=highest,
        preferred_element_type=jnp.float32,
    )
    for q in range(devs):
        part[q] = gram_part[q * chunk : (q + 1) * chunk, :]

    def slab(k):
        q = (d + k) % devs
        return q, place(g, q)

    def a_copy(k, incoming):
        q, to = slab(k)
        slot = (d + devs - k) % devs if incoming else d
        return copy(part.at[q], recv_a.at[slot], a_send.at[k], a_recv.at[k], to)

    for k in range(1, devs):
        a_copy(k, False).start()
    total = part[d]
    for k in range(1, devs):
        a_copy(k, True).wait_recv()
        total = total + recv_a[(d + devs - k) % devs]
    red[...] = total
    recv_b[g] = total

    def b_copy(k, incoming):
        _, to = peer(k)
        slot = (g + groups - k) % groups if incoming else g
        return copy(red, recv_b.at[slot], b_send.at[k], b_recv.at[k], to)

    for k in range(1, groups):
        b_copy(k, False).start()
    for s in range(1, server_rows):
        for k in range(1, groups):
            fc_copy(k, s, False).start()
    for k in range(1, groups):
        b_copy(k, True).wait_recv()
    total = recv_b[0]
    for q in range(1, groups):
        total = total + recv_b[q]
    tot[...] = total
    full[d] = total

    def c_copy(k, incoming):
        _, to = slab(k)
        slot = (d + devs - k) % devs if incoming else d
        return copy(tot, full.at[slot], c_send.at[k], c_recv.at[k], to)

    for k in range(1, devs):
        c_copy(k, False).start()
    for k in range(1, devs):
        c_copy(k, True).wait_recv()

    summed = jnp.concatenate([full[q] for q in range(devs)], axis=0)
    square = (members, members)
    diagonal = lax.broadcasted_iota(jnp.int32, square, 0) == lax.broadcasted_iota(
        jnp.int32, square, 1
    )
    identity = jnp.where(diagonal, 1.0, 0.0).astype(jnp.float32)
    gram = summed[:, :members] + (members - 1.0) * identity
    rhs = summed[:, members : members + 1]
    norm_total = jnp.sum(jnp.abs(gram))

    def dot(a, b):
        return jnp.dot(a, b, precision=highest, preferred_element_type=jnp.float32)

    def turn(_, pair):
        iterate, inverse = pair
        middle = 0.5 * (3.0 * identity - dot(inverse, iterate))
        return dot(iterate, middle), dot(middle, inverse)

    _, inverse = lax.fori_loop(0, NEWTON_STEPS, turn, (gram / norm_total, identity))
    right = jnp.broadcast_to(rhs, (members, LANES))
    shift = dot(inverse, dot(inverse, right)) / norm_total
    mix[...] = (jnp.sqrt((members - 1.0) / norm_total) * inverse + shift[:, 0:1]).T

    own_fc.wait()

    def centre(s, carry):
        for k in range(1, groups):
            fc_copy(k, s, True).wait_recv()
        block = gath[s]
        gath[s] = block - jnp.sum(block, axis=0, keepdims=True) / members
        return carry

    lax.fori_loop(0, server_rows, centre, 0)

    def out_copy(k, s, incoming):
        p, to = peer(k)
        slot = (g + groups - k) % groups if incoming else g
        return copy(
            send_buf.at[k, s], res.at[slot, s], out_send.at[k, s], out_recv.at[k, s], to
        )

    def mixed(p, s):
        weights = mix[pl.ds(pl.multiple_of(p * share, SUBLANES), share), :]
        return dot(weights, gath[s])

    for k in range(1, groups):

        def send(s, carry):
            send_buf[k, s] = mixed(peer(k)[0], s)
            out_copy(k, s, False).start()
            return carry

        lax.fori_loop(0, server_rows, send, 0)

    def keep(s, carry):
        res[g, s] = mixed(g, s)
        return carry

    lax.fori_loop(0, server_rows, keep, 0)

    for k in range(1, groups):
        proj_copy(k, False).wait_send()
        b_copy(k, False).wait_send()
        for s in range(server_rows):
            fc_copy(k, s, False).wait_send()
    for k in range(1, devs):
        a_copy(k, False).wait_send()
        c_copy(k, False).wait_send()
    for k in range(1, groups):
        for s in range(server_rows):
            out_copy(k, s, False).wait_send()
            out_copy(k, s, True).wait_recv()


def body(groups, devs, heads, soil_index, ks_table, alpha_table, obs_op, obs_mask, obs_values):
    soil = soil_values(soil_index, ks_table, alpha_table)
    mask = obs_mask.astype(jnp.float32)
    weights = (obs_op * mask[:, :, None, None]).reshape(-1, obs_op.shape[-1])
    values = (obs_values * mask[:, :, None]).reshape(1, -1)
    share, rows, columns = heads.shape
    server_rows = rows // groups
    observations = weights.shape[0]
    members = groups * share
    vmem = pl.BlockSpec(memory_space=pltpu.VMEM)
    anywhere = pl.BlockSpec(memory_space=pl.ANY)
    dma = pltpu.SemaphoreType.DMA
    f32 = jnp.float32
    extended = rows + 2 * MODEL_STEPS

    fc, proj = pl.pallas_call(
        functools.partial(forecast_kernel, groups, devs),
        out_shape=(
            jax.ShapeDtypeStruct((rows, share, columns), f32),
            jax.ShapeDtypeStruct((groups, share, observations), f32),
        ),
        in_specs=[anywhere] * 3,
        out_specs=(vmem, vmem),
        scratch_shapes=[
            pltpu.VMEM((extended, share, columns), f32),
            pltpu.VMEM((extended, share, columns), f32),
            pltpu.VMEM((extended, 2, columns), f32),
            pltpu.VMEM((groups, observations, LANES), f32),
            dma((3,)),
            dma((groups,)),
            dma((groups,)),
            dma((2,)),
            dma((2,)),
            dma((2,)),
            dma((2,)),
        ],
        compiler_params=pltpu.CompilerParams(collective_id=0, has_side_effects=True),
        name="forecast",
    )(heads.transpose(1, 0, 2), soil, weights)

    chunk = members // devs
    wide = (members // LANES + 1) * LANES
    res = pl.pallas_call(
        functools.partial(analysis_kernel, groups, devs),
        out_shape=jax.ShapeDtypeStruct((groups, server_rows, share, columns), f32),
        in_specs=[anywhere, anywhere, vmem],
        out_specs=vmem,
        scratch_shapes=[
            pltpu.VMEM((groups, share, observations), f32),
            pltpu.VMEM((server_rows, members, columns), f32),
            pltpu.VMEM((devs, chunk, wide), f32),
            pltpu.VMEM((devs, chunk, wide), f32),
            pltpu.VMEM((chunk, wide), f32),
            pltpu.VMEM((groups, chunk, wide), f32),
            pltpu.VMEM((chunk, wide), f32),
            pltpu.VMEM((devs, chunk, wide), f32),
            pltpu.VMEM((members, members), f32),
            pltpu.VMEM((groups, server_rows, share, columns), f32),
            dma((2,)),
            dma((groups,)),
            dma((groups,)),
            dma((groups, server_rows)),
            dma((groups, server_rows)),
            dma((devs,)),
            dma((devs,)),
            dma((groups,)),
            dma((groups,)),
            dma((devs,)),
            dma((devs,)),
            dma((groups, server_rows)),
            dma((groups, server_rows)),
        ],
        compiler_params=pltpu.CompilerParams(collective_id=1, has_side_effects=True),
        name="analysis",
    )(proj, fc.reshape(groups, server_rows, share, columns), values)
    return res.reshape(rows, share, columns).transpose(1, 0, 2)


def solution(mesh):
    groups, devs = mesh.shape["group"], mesh.shape["dev"]
    placed = (
        P("group", "dev", None),
        P("dev", None),
        P(),
        P(),
        P(("dev", "group"), None, None, None),
        P(("dev", "group"), None),
        P(("dev", "group"), None, None),
    )
    return jax.shard_map(
        functools.partial(body, groups, devs),
        mesh=mesh,
        in_specs=placed,
        out_specs=P("group", "dev", None),
        check_vma=False,
    )
```

```python
import functools

import jax
import jax.numpy as jnp
from jax import lax
from jax.experimental import pallas as pl
from jax.experimental.pallas import tpu as pltpu
from jax.sharding import PartitionSpec as P

MODEL_STEPS = 3
NEWTON_STEPS = 12
LANES = 128
SUBLANES = 8

step_duration = 0.1
gravity_head = 1.0
highest = lax.Precision.HIGHEST
MESH = pl.DeviceIdType.MESH
last_dims = (((1,), (1,)), ((), ()))


def soil_values(soil_index, ks_table, alpha_table):
    soil_kinds = jnp.arange(ks_table.shape[0], dtype=jnp.int32)
    one_hot = (soil_index[None] == soil_kinds[:, None, None]).astype(jnp.float32)
    return jnp.stack(
        [
            jnp.sum(one_hot * ks_table[:, None, None], axis=0),
            jnp.sum(one_hot * alpha_table[:, None, None], axis=0),
        ],
        axis=1,
    )


def place(group, dev):
    return {"group": group, "dev": dev}


def forecast_kernel(
    groups, devs, heads, soil, obs, fc, proj,
    ext_a, ext_b, soil_ext, obs_all,
    row_sem, local_sem, obs_send, obs_recv, halo_send, halo_recv, soil_send, soil_recv,
):
    w = MODEL_STEPS
    members, rows, columns = heads.shape
    blocks = columns // LANES
    server_rows = rows // groups
    g = lax.axis_index("group")
    d = lax.axis_index("dev")
    first, last = d == 0, d == devs - 1

    own_rows = [
        pltpu.make_async_copy(heads.at[:, r, :], ext_a.at[w + r], row_sem.at[r])
        for r in range(rows)
    ]
    own_soil = pltpu.make_async_copy(soil, soil_ext.at[pl.ds(w, rows)], local_sem.at[1])
    own_obs = pltpu.make_async_copy(obs, obs_all.at[g], local_sem.at[2])
    for c in own_rows:
        c.start()
    own_soil.start()
    own_obs.start()

    barrier = pltpu.get_barrier_semaphore()
    for k in range(1, groups):
        pl.semaphore_signal(
            barrier, inc=1, device_id=place((g + k) % groups, d), device_id_type=MESH
        )

    @pl.when(d > 0)
    def _():
        pl.semaphore_signal(barrier, inc=1, device_id=place(g, d - 1), device_id_type=MESH)

    @pl.when(d < devs - 1)
    def _():
        pl.semaphore_signal(barrier, inc=1, device_id=place(g, d + 1), device_id_type=MESH)

    neighbours = (d > 0).astype(jnp.int32) + (d < devs - 1).astype(jnp.int32)
    pl.semaphore_wait(barrier, groups - 1 + neighbours)

    for c in own_rows:
        c.wait()

    def halo(source, target, send, recv, side, base):
        start, put, to = ((base, w + rows, d - 1), (base + rows - w, 0, d + 1))[side]
        return pltpu.make_async_remote_copy(
            src_ref=source.at[pl.ds(start, w)],
            dst_ref=target.at[pl.ds(put, w)],
            send_sem=send.at[side],
            recv_sem=recv.at[side],
            device_id=place(g, to),
            device_id_type=MESH,
        )

    def halos(side):
        return (
            halo(soil, soil_ext, soil_send, soil_recv, side, 0),
            halo(ext_a, ext_a, halo_send, halo_recv, side, w),
        )

    @pl.when(d > 0)
    def _():
        for c in halos(0):
            c.start()

    @pl.when(d < devs - 1)
    def _():
        for c in halos(1):
            c.start()

    def obs_copy(k):
        return pltpu.make_async_remote_copy(
            src_ref=obs,
            dst_ref=obs_all.at[g],
            send_sem=obs_send.at[k],
            recv_sem=obs_recv.at[k],
            device_id=place((g + k) % groups, d),
            device_id_type=MESH,
        )

    def obs_arrival(k):
        return pltpu.make_async_remote_copy(
            src_ref=obs,
            dst_ref=obs_all.at[(g + groups - k) % groups],
            send_sem=obs_send.at[k],
            recv_sem=obs_recv.at[k],
            device_id=place((g + k) % groups, d),
            device_id_type=MESH,
        )

    for k in range(1, groups):
        obs_copy(k).start()

    def advance(src, dst, out_shift, low, high):
        def chunk(c, carry):
            part = pl.ds(pl.multiple_of(c * SUBLANES, SUBLANES), SUBLANES)
            shape = (SUBLANES, columns)
            lane = lax.broadcasted_iota(jnp.int32, shape, 1)
            has_next = lane < columns - 1
            has_before = lane > 0

            def law(i):
                h = src[i, part, :]
                ks = jnp.broadcast_to(soil_ext[i, 0:1, :], shape)
                alpha = jnp.broadcast_to(soil_ext[i, 1:2, :], shape)
                factor = jnp.exp(alpha * jnp.minimum(h, 0.0))
                return h, ks * factor, 0.1 + 0.4 * alpha * factor

            def across(h, k, h_next, k_next):
                return 0.5 * (k + k_next) * (h_next - h)

            h0, k0, _ = law(low - 1)
            h1, k1, c1 = law(low)

            def row(i, state):
                h, k, cap, g_before = state
                h_next, k_next, cap_next = law(i + 1)
                g_now = across(h, k, h_next, k_next)
                h_right = pltpu.roll(h, columns - 1, 1)
                k_right = pltpu.roll(k, columns - 1, 1)
                f = 0.5 * (k + k_right) * (h_right - h - gravity_head)
                f = jnp.where(has_next, f, 0.0)
                f_left = 0.5 * (k + pltpu.roll(k, 1, 1)) * (h - pltpu.roll(h, 1, 1) - gravity_head)
                f_left = jnp.where(has_before, f_left, 0.0)
                inflow = (g_now - g_before) + (f - f_left)
                dst[i - out_shift, part, :] = h + step_duration * inflow / cap
                return h_next, k_next, cap_next, g_now

            lax.fori_loop(low, high, row, (h1, k1, c1, across(h0, k0, h1, k1)), unroll=4)
            return carry

        lax.fori_loop(0, members // SUBLANES, chunk, 0)

    def clear(ref, low, high):
        ref[low:high] = jnp.zeros((high - low,) + ref.shape[1:], jnp.float32)

    own_soil.wait()

    advance(ext_a, ext_b, 0, w + 1, w + rows - 1)

    @pl.when(d > 0)
    def _():
        for c in halos(0):
            c.wait_send()
        for c in halos(1):
            c.wait_recv()

    @pl.when(d < devs - 1)
    def _():
        for c in halos(1):
            c.wait_send()
        for c in halos(0):
            c.wait_recv()

    @pl.when(first)
    def _():
        clear(ext_a, 0, w)
        clear(soil_ext, 0, w)

    @pl.when(last)
    def _():
        clear(ext_a, w + rows, rows + 2 * w)
        clear(soil_ext, w + rows, rows + 2 * w)

    advance(ext_a, ext_b, 0, 1, w + 1)
    advance(ext_a, ext_b, 0, w + rows - 1, rows + 2 * w - 1)

    def outside(ref, low, high):
        @pl.when(first)
        def _():
            clear(ref, low, w)

        @pl.when(last)
        def _():
            clear(ref, w + rows, high)

    outside(ext_b, 1, rows + 2 * w - 1)
    advance(ext_b, ext_a, 0, 2, rows + 2 * w - 2)
    outside(ext_a, 2, rows + 2 * w - 2)
    advance(ext_a, fc, w, w, w + rows)

    own_obs.wait()
    for k in range(1, groups):
        obs_copy(k).wait_send()
        obs_arrival(k).wait_recv()

    width = obs_all.shape[1] // server_rows
    per_block = width // blocks
    pairs = 2
    halves = server_rows // pairs

    def project(t, carry):
        owner, half = t // halves, t % halves
        pieces = []
        for p in range(pairs):
            r = t * pairs + p
            for b in range(blocks):
                weights = obs_all[
                    owner,
                    pl.ds(
                        pl.multiple_of(((half * pairs + p) * blocks + b) * per_block, SUBLANES),
                        per_block,
                    ),
                    :,
                ]
                pieces.append(
                    lax.dot_general(
                        fc[r, :, b * LANES : (b + 1) * LANES],
                        weights,
                        last_dims,
                        precision=highest,
                        preferred_element_type=jnp.float32,
                    )
                )
        proj[owner, :, pl.ds(pl.multiple_of(half * pairs * width, LANES), pairs * width)] = (
            jnp.concatenate(pieces, axis=1)
        )
        return carry

    lax.fori_loop(0, rows // pairs, project, 0)


def analysis_kernel(
    groups, devs, proj, fc, values, res,
    proj_all, gath, part, recv_a, red, recv_b, tot, full, mix, send_buf,
    local_sem, proj_send, proj_recv, fc_send, fc_recv,
    a_send, a_recv, b_send, b_recv, c_send, c_recv, out_send, out_recv,
):
    g = lax.axis_index("group")
    d = lax.axis_index("dev")
    _, server_rows, share, columns = fc.shape
    members = groups * share
    chunk = members // devs

    own_fc = pltpu.make_async_copy(
        fc.at[g], gath.at[:, pl.ds(pl.multiple_of(g * share, SUBLANES), share), :], local_sem.at[0]
    )
    own_proj = pltpu.make_async_copy(proj.at[g], proj_all.at[g], local_sem.at[1])
    own_fc.start()
    own_proj.start()

    barrier = pltpu.get_barrier_semaphore()
    for k in range(1, groups):
        pl.semaphore_signal(
            barrier, inc=1, device_id=place((g + k) % groups, d), device_id_type=MESH
        )
    for k in range(1, devs):
        pl.semaphore_signal(
            barrier, inc=1, device_id=place(g, (d + k) % devs), device_id_type=MESH
        )
    pl.semaphore_wait(barrier, groups - 1 + devs - 1)

    def copy(src, dst, send, recv, to):
        return pltpu.make_async_remote_copy(
            src_ref=src, dst_ref=dst, send_sem=send, recv_sem=recv,
            device_id=to, device_id_type=MESH,
        )

    def peer(k):
        p = (g + k) % groups
        return p, place(p, d)

    def member_slot(p, s):
        return gath.at[s, pl.ds(pl.multiple_of(p * share, SUBLANES), share), :]

    def proj_copy(k, incoming):
        p, to = peer(k)
        slot = (g + groups - k) % groups if incoming else g
        return copy(proj.at[p], proj_all.at[slot], proj_send.at[k], proj_recv.at[k], to)

    def fc_copy(k, s, incoming):
        p, to = peer(k)
        slot = (g + groups - k) % groups if incoming else g
        return copy(fc.at[p, s], member_slot(slot, s), fc_send.at[k, s], fc_recv.at[k, s], to)

    for k in range(1, groups):
        proj_copy(k, False).start()
    for k in range(1, groups):
        fc_copy(k, 0, False).start()
    own_proj.wait()
    for k in range(1, groups):
        proj_copy(k, True).wait_recv()

    observed = jnp.concatenate([proj_all[q] for q in range(groups)], axis=0)
    average = jnp.sum(observed, axis=0, keepdims=True) / members
    centred = observed - average
    innovation = values[...] - average
    extra = full.shape[2] - members
    padding = jnp.concatenate(
        [innovation, jnp.zeros((extra - 1, innovation.shape[1]), jnp.float32)], axis=0
    )
    gram_part = lax.dot_general(
        centred,
        jnp.concatenate([centred, padding], axis=0),
        last_dims,
        precision=highest,
        preferred_element_type=jnp.float32,
    )
    for q in range(devs):
        part[q] = gram_part[q * chunk : (q + 1) * chunk, :]

    def slab(k):
        q = (d + k) % devs
        return q, place(g, q)

    def a_copy(k, incoming):
        q, to = slab(k)
        slot = (d + devs - k) % devs if incoming else d
        return copy(part.at[q], recv_a.at[slot], a_send.at[k], a_recv.at[k], to)

    for k in range(1, devs):
        a_copy(k, False).start()
    total = part[d]
    for k in range(1, devs):
        a_copy(k, True).wait_recv()
        total = total + recv_a[(d + devs - k) % devs]
    red[...] = total
    recv_b[g] = total

    def b_copy(k, incoming):
        _, to = peer(k)
        slot = (g + groups - k) % groups if incoming else g
        return copy(red, recv_b.at[slot], b_send.at[k], b_recv.at[k], to)

    for k in range(1, groups):
        b_copy(k, False).start()
    for s in range(1, server_rows):
        for k in range(1, groups):
            fc_copy(k, s, False).start()
    for k in range(1, groups):
        b_copy(k, True).wait_recv()
    total = recv_b[0]
    for q in range(1, groups):
        total = total + recv_b[q]
    tot[...] = total
    full[d] = total

    def c_copy(k, incoming):
        _, to = slab(k)
        slot = (d + devs - k) % devs if incoming else d
        return copy(tot, full.at[slot], c_send.at[k], c_recv.at[k], to)

    for k in range(1, devs):
        c_copy(k, False).start()
    for k in range(1, devs):
        c_copy(k, True).wait_recv()

    summed = jnp.concatenate([full[q] for q in range(devs)], axis=0)
    square = (members, members)
    diagonal = lax.broadcasted_iota(jnp.int32, square, 0) == lax.broadcasted_iota(
        jnp.int32, square, 1
    )
    identity = jnp.where(diagonal, 1.0, 0.0).astype(jnp.float32)
    gram = summed[:, :members] + (members - 1.0) * identity
    rhs = summed[:, members : members + 1]
    norm_total = jnp.sum(jnp.abs(gram))

    def dot(a, b):
        return jnp.dot(a, b, precision=highest, preferred_element_type=jnp.float32)

    def turn(_, pair):
        iterate, inverse = pair
        middle = 0.5 * (3.0 * identity - dot(inverse, iterate))
        both = dot(jnp.concatenate([iterate, inverse], axis=0), middle)
        return both[:members], both[members:]

    scaled = gram / norm_total
    middle = 0.5 * (3.0 * identity - scaled)
    iterate, inverse = lax.fori_loop(
        0, NEWTON_STEPS - 2, turn, (dot(scaled, middle), middle)
    )
    inverse = dot(0.5 * (3.0 * identity - dot(inverse, iterate)), inverse)
    right = jnp.broadcast_to(rhs, (members, LANES))
    shift = dot(inverse, dot(inverse, right)) / norm_total
    mix[...] = (jnp.sqrt((members - 1.0) / norm_total) * inverse + shift[:, 0:1]).T

    own_fc.wait()

    def centre(s, carry):
        for k in range(1, groups):
            fc_copy(k, s, True).wait_recv()
        block = gath[s]
        gath[s] = block - jnp.sum(block, axis=0, keepdims=True) / members
        return carry

    lax.fori_loop(0, server_rows, centre, 0)

    def out_copy(k, s, incoming):
        p, to = peer(k)
        slot = (g + groups - k) % groups if incoming else g
        return copy(
            send_buf.at[k, s], res.at[slot, s], out_send.at[k, s], out_recv.at[k, s], to
        )

    def mixed(p, s):
        weights = mix[pl.ds(pl.multiple_of(p * share, SUBLANES), share), :]
        return dot(weights, gath[s])

    for k in range(1, groups):

        def send(s, carry):
            send_buf[k, s] = mixed(peer(k)[0], s)
            out_copy(k, s, False).start()
            return carry

        lax.fori_loop(0, server_rows, send, 0)

    def keep(s, carry):
        res[g, s] = mixed(g, s)
        return carry

    lax.fori_loop(0, server_rows, keep, 0)

    for k in range(1, groups):
        proj_copy(k, False).wait_send()
        b_copy(k, False).wait_send()
        for s in range(server_rows):
            fc_copy(k, s, False).wait_send()
    for k in range(1, devs):
        a_copy(k, False).wait_send()
        c_copy(k, False).wait_send()
    for k in range(1, groups):
        for s in range(server_rows):
            out_copy(k, s, False).wait_send()
            out_copy(k, s, True).wait_recv()


def body(groups, devs, heads, soil_index, ks_table, alpha_table, obs_op, obs_mask, obs_values):
    soil = soil_values(soil_index, ks_table, alpha_table)
    mask = obs_mask.astype(jnp.float32)
    weights = (obs_op * mask[:, :, None, None]).reshape(-1, obs_op.shape[-1])
    values = (obs_values * mask[:, :, None]).reshape(1, -1)
    share, rows, columns = heads.shape
    server_rows = rows // groups
    observations = weights.shape[0]
    members = groups * share
    vmem = pl.BlockSpec(memory_space=pltpu.VMEM)
    anywhere = pl.BlockSpec(memory_space=pl.ANY)
    dma = pltpu.SemaphoreType.DMA
    f32 = jnp.float32
    extended = rows + 2 * MODEL_STEPS

    fc, proj = pl.pallas_call(
        functools.partial(forecast_kernel, groups, devs),
        out_shape=(
            jax.ShapeDtypeStruct((rows, share, columns), f32),
            jax.ShapeDtypeStruct((groups, share, observations), f32),
        ),
        in_specs=[anywhere] * 3,
        out_specs=(vmem, vmem),
        scratch_shapes=[
            pltpu.VMEM((extended, share, columns), f32),
            pltpu.VMEM((extended, share, columns), f32),
            pltpu.VMEM((extended, 2, columns), f32),
            pltpu.VMEM((groups, observations, LANES), f32),
            dma((rows,)),
            dma((3,)),
            dma((groups,)),
            dma((groups,)),
            dma((2,)),
            dma((2,)),
            dma((2,)),
            dma((2,)),
        ],
        compiler_params=pltpu.CompilerParams(collective_id=0, has_side_effects=True),
        name="forecast",
    )(heads, soil, weights)

    chunk = members // devs
    wide = (members // LANES + 1) * LANES
    res = pl.pallas_call(
        functools.partial(analysis_kernel, groups, devs),
        out_shape=jax.ShapeDtypeStruct((groups, server_rows, share, columns), f32),
        in_specs=[anywhere, anywhere, vmem],
        out_specs=vmem,
        scratch_shapes=[
            pltpu.VMEM((groups, share, observations), f32),
            pltpu.VMEM((server_rows, members, columns), f32),
            pltpu.VMEM((devs, chunk, wide), f32),
            pltpu.VMEM((devs, chunk, wide), f32),
            pltpu.VMEM((chunk, wide), f32),
            pltpu.VMEM((groups, chunk, wide), f32),
            pltpu.VMEM((chunk, wide), f32),
            pltpu.VMEM((devs, chunk, wide), f32),
            pltpu.VMEM((members, members), f32),
            pltpu.VMEM((groups, server_rows, share, columns), f32),
            dma((2,)),
            dma((groups,)),
            dma((groups,)),
            dma((groups, server_rows)),
            dma((groups, server_rows)),
            dma((devs,)),
            dma((devs,)),
            dma((groups,)),
            dma((groups,)),
            dma((devs,)),
            dma((devs,)),
            dma((groups, server_rows)),
            dma((groups, server_rows)),
        ],
        compiler_params=pltpu.CompilerParams(collective_id=1, has_side_effects=True),
        name="analysis",
    )(proj, fc.reshape(groups, server_rows, share, columns), values)
    return res.reshape(rows, share, columns).transpose(1, 0, 2)


def solution(mesh):
    groups, devs = mesh.shape["group"], mesh.shape["dev"]
    placed = (
        P("group", "dev", None),
        P("dev", None),
        P(),
        P(),
        P(("dev", "group"), None, None, None),
        P(("dev", "group"), None),
        P(("dev", "group"), None, None),
    )
    return jax.shard_map(
        functools.partial(body, groups, devs),
        mesh=mesh,
        in_specs=placed,
        out_specs=P("group", "dev", None),
        check_vma=False,
    )
```
